128 devices in a mesh: trainer: 16 (over x, y_hi, core), depth: 8 (over y_lo, z).
Axes of the slice: x: 4, y: 4 (y_hi: 2, y_lo: 2; y = y_hi * 2 + y_lo), z: 4, core: 2. Of those that a mesh axis runs over, the one named last changes fastest.
Arguments:
- latent: bfloat16 [16, 16, 16, 16, 256], P('trainer', 'depth'), may hold values from -6 to 6
- gen_first: float32 [16, 256, 8192], P('trainer', 'depth'), may hold values from -0.125 to 0.125
- gen_second: float32 [16, 128, 4096], P('trainer', 'depth'), may hold values from -0.1875 to 0.1875
- critic: bfloat16 [16, 4096, 128], P('trainer'), may hold values from -0.09375 to 0.09375
- partner: int32 [16], replicated, may hold values from 0 to 15, as said below
Outputs:
- judged: bfloat16 [16, 2, 32, 32, 32, 128], P('trainer', None, 'depth')
The draws below stay inside these ranges and needn't reach their ends.
Inputs may be any that keep to these rules, and one draw needn't show every extreme that they name: partner[t] = t XOR m for every t, with one m for the whole array, 1 <= m < 16; so partner[partner[t]] = t and no trainer is its own partner.
All inputs are finite; a program needn't handle non-finite values.
Results may differ from the reference program's by a relative error of at most 0.0071.
Values may be sent and summed in bfloat16 or wider, within the bound.
No kernel may reach another device: no remote copies, remote signals or barrier semaphores. Data moves between devices by JAX's collectives and lax.ppermute only.
A program may use at most 128 MiB of HBM per device.

```python
import jax
import jax.numpy as jnp
from jax import lax

C0 = 256
C1 = 128
C2 = 64
C3 = 128
LAT_HW = 16
TRAINERS = 16
LAT_D = 16


def draw_partner(key, part):
    offset = jax.random.randint(key, (), 1, TRAINERS).astype(jnp.int32)
    return jnp.bitwise_xor(jnp.arange(TRAINERS, dtype=jnp.int32), offset)


def block_scale(own_key, shape, cuts, least, high):
    def one(axis_at, blocks):
        draws = jax.random.uniform(jax.random.fold_in(jax.random.fold_in(own_key, 6), axis_at), (blocks,), jnp.float32, least / len(cuts), high / len(cuts))
        return jnp.repeat(jnp.exp(draws), shape[axis_at] // blocks).reshape((-1,) + (1,) * (len(shape) - axis_at - 1))

    gain = one(*cuts[0])
    for cut in cuts[1:]:
        gain = gain * one(*cut)
    return gain


def bell_draw(key, extent, scale, reach, shards=(), kind=jnp.bfloat16):
    factor_of = block_scale(key, extent, shards, -0.22, 0.18) if shards else 1.0
    values = jax.random.normal(key, extent, jnp.float32) * scale * factor_of
    return jnp.minimum(jnp.maximum(values, -reach), reach).astype(kind)


def setup_inputs(seed: int = 0) -> dict:
    arg_keys = jax.random.split(jax.random.key(seed), 6)
    return {
        "latent": bell_draw(arg_keys[0], (TRAINERS, LAT_D, LAT_HW, LAT_HW, C0), 1.0, 6.0, ((0, 16), (1, 8))),
        "gen_first": bell_draw(arg_keys[1], (TRAINERS, C0, 64 * C1), (8 * C0) ** -0.5, 0.125, ((0, 16), (1, 8)), jnp.float32),
        "gen_second": bell_draw(arg_keys[2], (TRAINERS, C1, 64 * C2), (8 * C1) ** -0.5, 0.1875, ((0, 16), (1, 8)), jnp.float32),
        "critic": bell_draw(arg_keys[3], (TRAINERS, 64 * C2, C3), (64 * C2) ** -0.5, 0.09375, ((0, 16),)),
        "partner": draw_partner(jax.random.fold_in(arg_keys[5], 71), 0),
    }


leak_slope = 0.2


def product(left, right):
    return jnp.dot(left.astype(jnp.float32), right.astype(jnp.float32), precision=lax.Precision.HIGHEST, preferred_element_type=jnp.float32)


def alternate(blocks):
    stacked = jnp.stack([jnp.stack([jnp.stack(pair_w, 0) for pair_w in pair_h], 0) for pair_h in blocks], 0)
    planes, height, across, channels = blocks[0][0][0].shape
    reordered = jnp.transpose(stacked, (3, 0, 4, 1, 5, 2, 6))
    return reordered.reshape(2 * planes, 2 * height, 2 * across, channels)


def transposed(volume, kernel):
    planes = volume.shape[0] - 2
    height = volume.shape[1]
    across = volume.shape[2]
    in_channels = volume.shape[3]
    padded = jnp.pad(volume, ((0, 0), (1, 1), (1, 1), (0, 0)))
    flipped = jnp.flip(kernel, (0, 1, 2))
    blocks = []
    for along_depth in (0, 1):
        height_blocks = []
        for along_height in (0, 1):
            width_blocks = []
            for along_width in (0, 1):
                columns = []
                weights = []
                for depth_tap in (0, 1):
                    for height_tap in (0, 1):
                        for width_tap in (0, 1):
                            depth_start = along_depth + depth_tap
                            height_start = along_height + height_tap
                            width_start = along_width + width_tap
                            columns.append(padded[depth_start:depth_start + planes, height_start:height_start + height, width_start:width_start + across])
                            weights.append(flipped[along_depth + 2 * depth_tap, along_height + 2 * height_tap, along_width + 2 * width_tap])
                gathered = jnp.concatenate(columns, axis=3).reshape(-1, 8 * in_channels)
                stacked = jnp.concatenate(weights, axis=0)
                result = product(gathered, stacked)
                width_blocks.append(result.reshape(planes, height, across, -1))
            height_blocks.append(width_blocks)
        blocks.append(height_blocks)
    return alternate(blocks)


def strided(volume, kernel):
    out_planes = (volume.shape[0] - 2) // 2
    out_height = volume.shape[1] // 2
    out_across = volume.shape[2] // 2
    in_channels = volume.shape[3]
    padded = jnp.pad(volume, ((0, 0), (1, 1), (1, 1), (0, 0)))
    total = jnp.zeros((out_planes * out_height * out_across, kernel.shape[4]), jnp.float32)
    for depth_tap in range(4):
        for height_tap in range(4):
            columns = [padded[depth_tap:depth_tap + 2 * out_planes:2, height_tap:height_tap + 2 * out_height:2, width_tap:width_tap + 2 * out_across:2] for width_tap in range(4)]
            gathered = jnp.concatenate(columns, axis=3).reshape(-1, 4 * in_channels)
            total = total + product(gathered, kernel[depth_tap, height_tap].reshape(4 * in_channels, -1))
    return total.reshape(out_planes, out_height, out_across, -1)


def unfold(weight):
    in_channels = weight.shape[0]
    shaped = weight.reshape(in_channels, 4, 4, 4, weight.shape[1] // 64)
    return jnp.transpose(shaped, (1, 2, 3, 0, 4))


def pad_depth(volume):
    return jnp.pad(volume, ((1, 1), (0, 0), (0, 0), (0, 0)))


def generate(seed_planes, first_weight, second_weight):
    first_kernel = unfold(first_weight.astype(jnp.bfloat16))
    second_kernel = unfold(second_weight.astype(jnp.bfloat16))
    hidden = jnp.maximum(transposed(pad_depth(seed_planes), first_kernel), 0.0).astype(jnp.bfloat16)
    density = jnp.tanh(transposed(pad_depth(hidden), second_kernel)).astype(jnp.bfloat16)
    return density


def judge(density, critic_kernel):
    scored = strided(pad_depth(density), critic_kernel)
    return jnp.where(scored > 0, scored, leak_slope * scored).astype(jnp.bfloat16)


def reference(latent, gen_first, gen_second, critic, partner):
    def one_trainer(trainer_index):
        mate_index = partner[trainer_index]
        seed_planes = latent[trainer_index]
        critic_kernel = critic[trainer_index].reshape(4, 4, 4, C2, C3)
        own_density = generate(seed_planes, gen_first[trainer_index], gen_second[trainer_index])
        mate_density = generate(seed_planes, gen_first[mate_index], gen_second[mate_index])
        return jnp.stack([judge(own_density, critic_kernel), judge(mate_density, critic_kernel)])

    return lax.map(one_trainer, jnp.arange(TRAINERS, dtype=jnp.int32))
```

```python
import functools

import jax
import jax.numpy as jnp
from jax import lax
from jax.experimental import pallas as pl
from jax.experimental.pallas import tpu as pltpu
from jax.sharding import PartitionSpec as P

leak_slope = 0.2
bf16 = jnp.bfloat16
f32 = jnp.float32


def dot(a, b):
    return lax.dot_general(a, b, (((1,), (0,)), ((), ())), preferred_element_type=f32)


def eval_kernel(edge, x_ref, w1_ref, w2_ref, crit_ref, prev_ref, out_ref,
                xa, hp, hs0, hs1, d0, d1, zb, cr, cb, tmp):
    row3 = lambda n, lanes: lax.broadcasted_iota(jnp.int32, (n, 16, lanes), 1)
    del prev_ref

    for kd in range(4):
        for kh in range(4):
            g, sh = kh // 2, kh % 2
            for slot in range(2):
                kw = slot if sh == 0 else 1 - slot
                base = (kd * 4 + kh) * 256
                r0 = sh * 128 + slot * 64
                for half in range(2):
                    src = base + (half * 2 + kw) * 64
                    cr[kd * 2 + g, r0:r0 + 64, half * 128:half * 128 + 128] = crit_ref[src:src + 64, :]
            src = (kd * 4 + kh) * 256 + 128
            dst = (kd * 2 + g) * 128 + sh * 64
            cb[dst:dst + 64, :] = crit_ref[src:src + 64, :]

    zrow = jnp.zeros((16, 256), bf16)
    for v in range(4):
        for p in range(4):
            xa[v, p, 0] = zrow
            xa[v, p, 17] = zrow
    for p in range(4):
        x = x_ref[p].astype(f32)
        r = row3(16, 256)
        rolled = pltpu.roll(x, 1, 1)
        xa[0, p, 1:17] = rolled.astype(bf16)
        xa[1, p, 1:17] = jnp.where(r == 0, 0.0, x).astype(bf16)
        xa[2, p, 1:17] = jnp.where(r == 0, 0.0, rolled).astype(bf16)
        xa[3, p, 1:17] = x_ref[p]

    def first(jd, _):
        outs = []
        for sw in range(2):
            lhs, rhs = [], []
            for ed in range(2):
                for eh in range(2):
                    for ew in range(2):
                        lhs.append(xa[sw * 2 + ew, jd + ed, eh:eh + 17].reshape(272, 256))
                        cols = []
                        for sd in range(2):
                            for sh in range(2):
                                k = ((2 + sd - 2 * ed) * 4 + (2 + sh - 2 * eh)) * 4 + (2 + sw - 2 * ew)
                                cols.append(w1_ref[:, k * 128:k * 128 + 128])
                        rhs.append(jnp.concatenate(cols, axis=1))
            res = dot(jnp.concatenate(lhs, axis=1), jnp.concatenate(rhs, axis=0))
            outs.append(jnp.maximum(res, 0.0))
        r = row3(17, 128)
        for sd in range(2):
            for sh in range(2):
                lane = (sd * 2 + sh) * 128
                o0 = outs[0][:, lane:lane + 128].reshape(17, 16, 128)
                o1 = outs[1][:, lane:lane + 128].reshape(17, 16, 128)
                a0 = o0.astype(bf16)
                a1 = o1.astype(bf16)
                a0r = pltpu.roll(o0, 15, 1).astype(bf16)
                a0z = jnp.where(r == 0, 0.0, o0).astype(bf16)
                a1z = jnp.where(r == 0, 0.0, o1).astype(bf16)
                p = 2 * jd + sd
                for j in range(17):
                    h = 2 * j + sh
                    hp[p, h, :, 0:128] = a1[j]
                    hp[p, h, :, 128:256] = a0r[j]
                    hs0[p, h, :, 0:128] = a0[j]
                    hs0[p, h, :, 128:256] = a1z[j]
                    hs1[p, h, :, 0:128] = a0z[j]
                    hs1[p, h, :, 128:256] = a1[j]
        return 0

    lax.fori_loop(0, 3, first, 0)
    for h in (hp, hs0, hs1):
        for p in range(6):
            h[p, 0] = zrow
            h[p, 33] = zrow

    @pl.when(edge[0] == 1)
    def _():
        for h in (hp, hs0, hs1):
            h[0] = jnp.zeros((34, 16, 256), bf16)

    @pl.when(edge[1] == 1)
    def _():
        for h in (hp, hs0, hs1):
            h[5] = jnp.zeros((34, 16, 256), bf16)

    def second(jd, _):
        def rhs(s):
            parts = []
            for e in range(4):
                for ew in range(2):
                    c = ((e * 2 + ew) * 2 + s) * 256
                    parts.append(w2_ref[:, c:c + 256])
            return jnp.concatenate(parts, axis=0)

        def lhs(h):
            return jnp.concatenate(
                [h[jd + ed, eh:eh + 33].reshape(528, 256) for ed in range(2) for eh in range(2)], axis=1)

        lane = lax.broadcasted_iota(jnp.int32, (528, 128), 1)
        r = row3(33, 128)
        zr = lax.broadcasted_iota(jnp.int32, (33, 128), 0)
        zl = lax.broadcasted_iota(jnp.int32, (33, 128), 1)
        for a in range(2):
            dst = d0 if a == 0 else d1
            t0 = jnp.tanh(dot(lhs(hs0 if a == 0 else hp), rhs(0)))
            t1 = jnp.tanh(dot(lhs(hs1 if a == 0 else hp), rhs(1)))
            for sd in range(2):
                p = 2 * jd + sd
                u0 = t0[:, sd * 128:sd * 128 + 128]
                u1 = t1[:, sd * 128:sd * 128 + 128]
                if a == 0:
                    z = u0.reshape(33, 16, 128)[:, 0, :]
                    drop = ((zr == 0) & (zl < 64)) | ((zr == 32) & (zl >= 64))
                    zb[p, 0:33, :] = jnp.where(drop, 0.0, z)
                    u0 = jnp.where(r == 0, 0.0, u0.reshape(33, 16, 128)).reshape(528, 128)
                low = jnp.where(lane < 64, u0, u1).astype(bf16)
                high = jnp.where(lane < 64, u1, u0).astype(bf16)
                dst[p, :, :, 0:128] = low.reshape(33, 16, 128)
                dst[p, :, :, 128:256] = high.reshape(33, 16, 128)
        return 0

    lax.fori_loop(0, 5, second, 0)
    z128 = jnp.zeros((16, 128), bf16)
    for d in (d0, d1):
        for p in range(10):
            d[p, 0, :, 0:128] = z128
            d[p, 32, :, 128:256] = z128

    @pl.when(edge[0] == 1)
    def _():
        for d in (d0, d1):
            d[0] = jnp.zeros((33, 16, 256), bf16)
        zb[0] = jnp.zeros((40, 128), f32)

    @pl.when(edge[1] == 1)
    def _():
        for d in (d0, d1):
            d[9] = jnp.zeros((33, 16, 256), bf16)
        zb[9] = jnp.zeros((40, 128), f32)

    def judge(y, _):
        def lhs(d):
            return jnp.concatenate(
                [d[2 * y + kd, g:g + 32].reshape(512, 256) for kd in range(4) for g in range(2)], axis=1)

        w = cr[...].reshape(2048, 256)
        acc0 = dot(lhs(d0), w)
        acc1 = dot(lhs(d1), w)
        bl = jnp.concatenate(
            [zb[2 * y + kd, g:g + 32, :].astype(bf16) for kd in range(4) for g in range(2)], axis=1)
        past = dot(bl, cb[...])
        even = acc0[:, 0:128] + acc1[:, 128:256]
        side = pltpu.roll(acc0[:, 128:256].reshape(32, 16, 128), 15, 1)
        side = jnp.where(row3(32, 128) == 15, past[:, None, :], side)
        odd = acc1[:, 0:128] + side.reshape(512, 128)
        tmp[pl.ds(0, 512, 2), :] = jnp.where(even > 0, even, leak_slope * even)
        tmp[pl.ds(1, 512, 2), :] = jnp.where(odd > 0, odd, leak_slope * odd)
        out_ref[0, y] = tmp[...].astype(bf16).reshape(32, 32, 128)
        return 0

    lax.fori_loop(0, 4, judge, 0)


def evaluate(edge, planes, w1, w2, crit, prev, which, interpret=False):
    vm = pl.BlockSpec(memory_space=pltpu.VMEM)
    args = [edge, planes, w1, w2, crit]
    out_shape = jax.ShapeDtypeStruct((2, 4, 32, 32, 128), bf16)
    kernel = eval_kernel
    specs = [pl.BlockSpec(memory_space=pltpu.SMEM), vm, vm, vm, vm]
    alias = {}
    if prev is None:
        kernel = lambda *r: eval_kernel(*r[:5], None, *r[5:])
    else:
        args.append(prev)
        specs.append(pl.BlockSpec(memory_space=pl.ANY))
        alias = {5: 0}
    return pl.pallas_call(
        kernel,
        grid=(1,),
        in_specs=specs,
        out_specs=pl.BlockSpec((1, 4, 32, 32, 128), lambda i: (which, 0, 0, 0, 0)),
        out_shape=out_shape,
        input_output_aliases=alias,
        scratch_shapes=[
            pltpu.VMEM((4, 4, 18, 16, 256), bf16),
            pltpu.VMEM((6, 34, 16, 256), bf16),
            pltpu.VMEM((6, 34, 16, 256), bf16),
            pltpu.VMEM((6, 34, 16, 256), bf16),
            pltpu.VMEM((10, 33, 16, 256), bf16),
            pltpu.VMEM((10, 33, 16, 256), bf16),
            pltpu.VMEM((10, 40, 128), f32),
            pltpu.VMEM((8, 256, 256), bf16),
            pltpu.VMEM((1024, 128), bf16),
            pltpu.VMEM((1024, 128), f32),
        ],
        compiler_params=pltpu.CompilerParams(vmem_limit_bytes=60 << 20),
        interpret=interpret,
        name="evaluate",
    )(*args)


def arrange_second(shard):
    rows = shard.shape[0]
    v = shard.reshape(rows, 2, 2, 2, 2, 2, 2, 64)
    v = v[:, ::-1, :, ::-1, :, ::-1]
    v = jnp.transpose(v, (0, 1, 3, 5, 6, 2, 4, 7))
    v = jnp.stack([v[:, :, :, :, 0], v[:, :, :, :, 1, :, ::-1]], axis=4)
    return v.reshape(rows, 4096)


def shift(value, axis, step):
    count = lax.axis_size(axis)
    pairs = [(i, i + step) for i in range(count) if 0 <= i + step < count]
    return lax.ppermute(value, axis, pairs)


def swap_all(values, offset):
    count = lax.axis_size("trainer")

    def branch(m):
        pairs = [(i, i ^ m) for i in range(count)]
        return lambda v: jax.tree.map(lambda a: lax.ppermute(a, "trainer", pairs), v)

    return lax.switch(offset - 1, [branch(m) for m in range(1, count)], values)


def local(latent, gen_first, gen_second, critic, partner):
    offset = partner[0]
    depth = lax.axis_index("depth")
    last = lax.axis_size("depth") - 1
    edge = jnp.stack([(depth == 0).astype(jnp.int32), (depth == last).astype(jnp.int32)])
    first_shard = gen_first[0].astype(bf16)
    second_shard = arrange_second(gen_second[0].astype(bf16))
    gather = lambda v: lax.all_gather(v, "depth", axis=0, tiled=True)
    own_first, own_second = gather(first_shard), gather(second_shard)
    low = shift(latent[0, -1:], "depth", 1)
    high = shift(latent[0, :1], "depth", -1)
    planes = jnp.concatenate([low, latent[0], high], axis=0)
    mate_first_shard, mate_second_shard = swap_all((first_shard, second_shard), offset)
    mate_first, mate_second = gather(mate_first_shard), gather(mate_second_shard)
    own = evaluate(edge, planes, own_first, own_second, critic[0], None, 0)
    both = evaluate(edge, planes, mate_first, mate_second, critic[0], own, 1)
    return both[None]


def solution(mesh):
    in_specs = (
        P("trainer", "depth", None, None, None),
        P("trainer", "depth", None),
        P("trainer", "depth", None),
        P("trainer", None, None),
        P(),
    )
    out_specs = P("trainer", None, "depth", None, None, None)
    return jax.shard_map(local, mesh=mesh, in_specs=in_specs, out_specs=out_specs, check_vma=False)
```

```python
import jax
import jax.numpy as jnp
from jax import lax
from jax.experimental import pallas as pl
from jax.experimental.pallas import tpu as pltpu
from jax.sharding import PartitionSpec as P

leak_slope = 0.2
bf16 = jnp.bfloat16
f32 = jnp.float32


def dot(a, b):
    return lax.dot_general(a, b, (((1,), (0,)), ((), ())), preferred_element_type=f32)


c1, c2, wide = 3456, 6912, 10240


def prep_kernel(first_ref, second_ref, out_ref):
    out_ref[:, 0:8192] = first_ref[...].astype(bf16)
    lane = lax.broadcasted_iota(jnp.int32, (16, 128), 1)
    for block in range(32):
        ed, eh, ew, sw, sd = (block >> 4) & 1, (block >> 3) & 1, (block >> 2) & 1, (block >> 1) & 1, block & 1
        parts = []
        for slot in range(2):
            sh = slot if sw == 0 else 1 - slot
            k = ((2 + sd - 2 * ed) * 4 + (2 + sh - 2 * eh)) * 4 + (2 + sw - 2 * ew)
            v = second_ref[:, (k // 2) * 128:(k // 2) * 128 + 128]
            parts.append(v if k % 2 == slot else pltpu.roll(v, 64, 1))
        v = jnp.where(lane < 64, parts[0], parts[1]).astype(bf16)
        row, col = (block // 16) * 16, 8192 + (block % 16) * 128
        out_ref[row:row + 16, col:col + 128] = v


def pack(gen_first, gen_second, interpret=False):
    vm = pl.BlockSpec(memory_space=pltpu.VMEM)
    return pl.pallas_call(
        prep_kernel,
        in_specs=[vm, vm],
        out_specs=vm,
        out_shape=jax.ShapeDtypeStruct((32, wide), bf16),
        interpret=interpret,
        name="pack",
    )(gen_first, gen_second)


def piece_copies(idx, pieces, w1, w2):
    own, a1, a3, b0, q, r, s, t, u, w = pieces
    first, second = [], []

    def rows(src, src_row, count, shard, row):
        base = pl.multiple_of(idx[shard] * 32 + row, 16)
        first.append((src.at[pl.ds(src_row, count), pl.ds(0, 8192)], w1.at[pl.ds(base, count), :]))
        base = pl.multiple_of(idx[shard] * 16, 16)
        for part in range(count // 16):
            col = (row // 16 + part) * 2048
            second.append((src.at[pl.ds(src_row + 16 * part, 16), pl.ds(8192, 2048)],
                           w2.at[pl.ds(base, 16), pl.ds(col, 2048)]))

    for n, src in enumerate((own, a1, a3, b0)):
        rows(src, 0, 32, n, 0)
    rows(q, 0, 16, 4, 0)
    rows(r, 0, 16, 4, 16)
    rows(q, 16, 16, 5, 0)
    rows(s, 0, 16, 5, 16)
    rows(s, 16, 16, 6, 0)
    rows(r, 16, 16, 6, 16)
    base = pl.multiple_of(idx[7] * 32, 32)
    first.append((t, w1.at[pl.ds(base, 32), pl.ds(0, c1)]))
    first.append((u, w1.at[pl.ds(base, 32), pl.ds(c1, c2 - c1)]))
    first.append((w.at[:, pl.ds(0, 8192 - c2)], w1.at[pl.ds(base, 32), pl.ds(c2, 8192 - c2)]))
    base = pl.multiple_of(idx[7] * 16, 16)
    for part in range(2):
        second.append((w.at[pl.ds(16 * part, 16), pl.ds(8192 - c2, 2048)],
                       w2.at[pl.ds(base, 16), pl.ds(part * 2048, 2048)]))
    return first, second


def eval_kernel(idx, x_ref, crit_hbm, *refs):
    pieces, out_ref = refs[:10], refs[10]
    (w1_ref, w2_ref, crit_ref, xa, hp, hs0, hs1, d0, d1, zb, cr, cb, tmp, sem1, sem2, sem3) = refs[11:]
    edge = [idx[8], idx[9]]
    row3 = lambda n, lanes: lax.broadcasted_iota(jnp.int32, (n, 16, lanes), 1)

    first, second = piece_copies(idx, pieces, w1_ref, w2_ref)
    first = [pltpu.make_async_copy(a, b, sem1.at[n]) for n, (a, b) in enumerate(first)]
    second_copies = [pltpu.make_async_copy(a, b, sem2.at[n]) for n, (a, b) in enumerate(second)]
    crit_copy = pltpu.make_async_copy(crit_hbm, crit_ref, sem3.at[0])
    for c in first + second_copies + [crit_copy]:
        c.start()

    zrow = jnp.zeros((16, 256), bf16)
    for v in range(4):
        for p in range(4):
            xa[v, p, 0] = zrow
            xa[v, p, 17] = zrow
    for p in range(4):
        x = x_ref[p].astype(f32)
        r = row3(16, 256)
        rolled = pltpu.roll(x, 1, 1)
        xa[0, p, 1:17] = rolled.astype(bf16)
        xa[1, p, 1:17] = jnp.where(r == 0, 0.0, x).astype(bf16)
        xa[2, p, 1:17] = jnp.where(r == 0, 0.0, rolled).astype(bf16)
        xa[3, p, 1:17] = x_ref[p]

    for c in first:
        c.wait()

    def first_layer(jd, _):
        outs = []
        for sw in range(2):
            lhs, rhs = [], []
            for ed in range(2):
                for eh in range(2):
                    for ew in range(2):
                        lhs.append(xa[sw * 2 + ew, jd + ed, eh:eh + 17].reshape(272, 256))
                        cols = []
                        for sd in range(2):
                            for sh in range(2):
                                k = ((2 + sd - 2 * ed) * 4 + (2 + sh - 2 * eh)) * 4 + (2 + sw - 2 * ew)
                                cols.append(w1_ref[:, k * 128:k * 128 + 128])
                        rhs.append(jnp.concatenate(cols, axis=1))
            res = dot(jnp.concatenate(lhs, axis=1), jnp.concatenate(rhs, axis=0))
            outs.append(jnp.maximum(res, 0.0))
        r = row3(17, 128)
        for sd in range(2):
            for sh in range(2):
                lane = (sd * 2 + sh) * 128
                o0 = outs[0][:, lane:lane + 128].reshape(17, 16, 128)
                o1 = outs[1][:, lane:lane + 128].reshape(17, 16, 128)
                a0 = o0.astype(bf16)
                a1 = o1.astype(bf16)
                a0r = pltpu.roll(o0, 15, 1).astype(bf16)
                a0z = jnp.where(r == 0, 0.0, o0).astype(bf16)
                a1z = jnp.where(r == 0, 0.0, o1).astype(bf16)
                p = 2 * jd + sd
                for j in range(17):
                    h = 2 * j + sh
                    hp[p, h, :, 0:128] = a1[j]
                    hp[p, h, :, 128:256] = a0r[j]
                    hs0[p, h, :, 0:128] = a0[j]
                    hs0[p, h, :, 128:256] = a1z[j]
                    hs1[p, h, :, 0:128] = a0z[j]
                    hs1[p, h, :, 128:256] = a1[j]
        return 0

    lax.fori_loop(0, 3, first_layer, 0)
    for h in (hp, hs0, hs1):
        for p in range(6):
            h[p, 0] = zrow
            h[p, 33] = zrow

    @pl.when(edge[0] == 1)
    def _():
        for h in (hp, hs0, hs1):
            h[0] = jnp.zeros((34, 16, 256), bf16)

    @pl.when(edge[1] == 1)
    def _():
        for h in (hp, hs0, hs1):
            h[5] = jnp.zeros((34, 16, 256), bf16)

    for c in second_copies:
        c.wait()

    def second_layer(jd, _):
        def rhs(s):
            parts = []
            for e in range(4):
                for ew in range(2):
                    c = ((e * 2 + ew) * 2 + s) * 256
                    parts.append(w2_ref[:, c:c + 256])
            return jnp.concatenate(parts, axis=0)

        def lhs(h):
            return jnp.concatenate(
                [h[jd + ed, eh:eh + 33].reshape(528, 256) for ed in range(2) for eh in range(2)], axis=1)

        lane = lax.broadcasted_iota(jnp.int32, (528, 128), 1)
        r = row3(33, 128)
        zr = lax.broadcasted_iota(jnp.int32, (33, 128), 0)
        zl = lax.broadcasted_iota(jnp.int32, (33, 128), 1)
        for a in range(2):
            dst = d0 if a == 0 else d1
            t0 = jnp.tanh(dot(lhs(hs0 if a == 0 else hp), rhs(0)))
            t1 = jnp.tanh(dot(lhs(hs1 if a == 0 else hp), rhs(1)))
            for sd in range(2):
                p = 2 * jd + sd
                u0 = t0[:, sd * 128:sd * 128 + 128]
                u1 = t1[:, sd * 128:sd * 128 + 128]
                if a == 0:
                    z = u0.reshape(33, 16, 128)[:, 0, :]
                    drop = ((zr == 0) & (zl < 64)) | ((zr == 32) & (zl >= 64))
                    zb[p, 0:33, :] = jnp.where(drop, 0.0, z)
                    u0 = jnp.where(r == 0, 0.0, u0.reshape(33, 16, 128)).reshape(528, 128)
                low = jnp.where(lane < 64, u0, u1).astype(bf16)
                high = jnp.where(lane < 64, u1, u0).astype(bf16)
                dst[p, :, :, 0:128] = low.reshape(33, 16, 128)
                dst[p, :, :, 128:256] = high.reshape(33, 16, 128)
        return 0

    lax.fori_loop(0, 5, second_layer, 0)
    crit_copy.wait()
    for kd in range(4):
        for kh in range(4):
            g, sh = kh // 2, kh % 2
            for slot in range(2):
                kw = slot if sh == 0 else 1 - slot
                base = (kd * 4 + kh) * 256
                r0 = sh * 128 + slot * 64
                for half in range(2):
                    src = base + (half * 2 + kw) * 64
                    cr[kd * 2 + g, r0:r0 + 64, half * 128:half * 128 + 128] = crit_ref[src:src + 64, :]
            src = (kd * 4 + kh) * 256 + 128
            dst = (kd * 2 + g) * 128 + sh * 64
            cb[dst:dst + 64, :] = crit_ref[src:src + 64, :]
    z128 = jnp.zeros((16, 128), bf16)
    for d in (d0, d1):
        for p in range(10):
            d[p, 0, :, 0:128] = z128
            d[p, 32, :, 128:256] = z128

    @pl.when(edge[0] == 1)
    def _():
        for d in (d0, d1):
            d[0] = jnp.zeros((33, 16, 256), bf16)
        zb[0] = jnp.zeros((40, 128), f32)

    @pl.when(edge[1] == 1)
    def _():
        for d in (d0, d1):
            d[9] = jnp.zeros((33, 16, 256), bf16)
        zb[9] = jnp.zeros((40, 128), f32)

    def judge(y, _):
        def lhs(d):
            return jnp.concatenate(
                [d[2 * y + kd, g:g + 32].reshape(512, 256) for kd in range(4) for g in range(2)], axis=1)

        w = cr[...].reshape(2048, 256)
        acc0 = dot(lhs(d0), w)
        acc1 = dot(lhs(d1), w)
        bl = jnp.concatenate(
            [zb[2 * y + kd, g:g + 32, :].astype(bf16) for kd in range(4) for g in range(2)], axis=1)
        past = dot(bl, cb[...])
        even = acc0[:, 0:128] + acc1[:, 128:256]
        side = pltpu.roll(acc0[:, 128:256].reshape(32, 16, 128), 15, 1)
        side = jnp.where(row3(32, 128) == 15, past[:, None, :], side)
        odd = acc1[:, 0:128] + side.reshape(512, 128)
        tmp[pl.ds(0, 512, 2), :] = jnp.where(even > 0, even, leak_slope * even)
        tmp[pl.ds(1, 512, 2), :] = jnp.where(odd > 0, odd, leak_slope * odd)
        out_ref[0, y] = tmp[...].astype(bf16).reshape(32, 32, 128)
        return 0

    lax.fori_loop(0, 4, judge, 0)


def evaluate(idx, planes, crit, pieces, halves, interpret=False):
    vm = pl.BlockSpec(memory_space=pltpu.VMEM)
    hbm = pl.BlockSpec(memory_space=pl.ANY)
    return pl.pallas_call(
        eval_kernel,
        grid=(1,),
        in_specs=[pl.BlockSpec(memory_space=pltpu.SMEM), vm, hbm] + [hbm] * 10,
        out_specs=pl.BlockSpec((1, 4, 32, 32, 128), lambda i: (0, 0, 0, 0, 0)),
        out_shape=jax.ShapeDtypeStruct((halves, 4, 32, 32, 128), bf16),
        scratch_shapes=[
            pltpu.VMEM((256, 8192), bf16),
            pltpu.VMEM((128, 4096), bf16),
            pltpu.VMEM((4096, 128), bf16),
            pltpu.VMEM((4, 4, 18, 16, 256), bf16),
            pltpu.VMEM((6, 34, 16, 256), bf16),
            pltpu.VMEM((6, 34, 16, 256), bf16),
            pltpu.VMEM((6, 34, 16, 256), bf16),
            pltpu.VMEM((10, 33, 16, 256), bf16),
            pltpu.VMEM((10, 33, 16, 256), bf16),
            pltpu.VMEM((10, 40, 128), f32),
            pltpu.VMEM((8, 256, 256), bf16),
            pltpu.VMEM((1024, 128), bf16),
            pltpu.VMEM((1024, 128), f32),
            pltpu.SemaphoreType.DMA((13,)),
            pltpu.SemaphoreType.DMA((16,)),
            pltpu.SemaphoreType.DMA((1,)),
        ],
        compiler_params=pltpu.CompilerParams(vmem_limit_bytes=60 << 20),
        interpret=interpret,
        name="evaluate",
    )(idx, planes, crit, *pieces)


def shift(value, axis, step):
    count = lax.axis_size(axis)
    pairs = [(i, i + step) for i in range(count) if 0 <= i + step < count]
    return lax.ppermute(value, axis, pairs)


def across(offset, make, *values):
    count = lax.axis_size("trainer")

    def branch(m):
        pairs = [(i, i ^ m) for i in range(count)]
        send = lambda v: jax.tree.map(lambda a: lax.ppermute(a, "trainer", pairs), v)
        return lambda *v: make(send, *v)

    return lax.switch(offset - 1, [branch(m) for m in range(1, count)], *values)


def gather_pieces(own):
    ring = lambda v, step: lax.ppermute(v, "depth", [(i, (i & 4) | ((i + step) & 3)) for i in range(8)])
    other = lambda v: lax.ppermute(v, "depth", [(i, i ^ 4) for i in range(8)])
    cat = lambda *v: jnp.concatenate(v, axis=0)
    a1, a3, b0 = ring(own, 1), ring(own, -1), other(own)
    yield
    q = ring(cat(a1[:16], b0[:16]), 1)
    r = ring(cat(a3[16:], b0[16:]), -1)
    s = other(cat(a1[16:], a3[:16]))
    yield
    t = ring(cat(q[16:, :c1], s[:16, :c1]), 1)
    u = ring(cat(s[16:, c1:c2], r[16:, c1:c2]), -1)
    w = other(cat(q[:16, c2:], r[:16, c2:]))
    yield own, a1, a3, b0, q, r, s, t, u, w


def local(latent, gen_first, gen_second, critic, partner):
    offset = partner[0]
    depth = lax.axis_index("depth")
    last = lax.axis_size("depth") - 1
    row, at = depth & 4, depth & 3
    a1, a3, a2 = row | ((at + 3) & 3), row | ((at + 1) & 3), row | ((at + 2) & 3)
    idx = jnp.stack([depth, a1, a3, depth ^ 4, a2, a1 ^ 4, a3 ^ 4, a2 ^ 4,
                     (depth == 0).astype(jnp.int32), (depth == last).astype(jnp.int32)])
    rounds = gather_pieces(pack(gen_first[0], gen_second[0]))
    next(rounds)
    low = shift(latent[0, -1:], "depth", 1)
    high = shift(latent[0, :1], "depth", -1)
    planes = jnp.concatenate([low, latent[0], high], axis=0)
    crit = critic[0]
    cut = 2560
    just_send = lambda send, *v: send(v)
    (mate_crit_low,) = across(offset, just_send, crit[:cut])
    next(rounds)
    mate_planes, mate_crit_high = across(offset, just_send, planes, crit[cut:])
    pieces = next(rounds)
    mate_crit = jnp.concatenate([mate_crit_low, mate_crit_high], axis=0)
    for_mate = evaluate(idx, mate_planes, mate_crit, pieces, 1)

    def finish(send, for_mate, idx, planes, crit, pieces):
        return send(for_mate), evaluate(idx, planes, crit, pieces, 2)

    mine, out = across(offset, finish, for_mate, idx, planes, crit, pieces)
    return lax.dynamic_update_slice_in_dim(out, mine, 1, 0)[None]


def solution(mesh):
    in_specs = (
        P("trainer", "depth", None, None, None),
        P("trainer", "depth", None),
        P("trainer", "depth", None),
        P("trainer", None, None),
        P(),
    )
    out_specs = P("trainer", None, "depth", None, None, None)
    return jax.shard_map(local, mesh=mesh, in_specs=in_specs, out_specs=out_specs, check_vma=False)
```

```python
import jax
import jax.numpy as jnp
from jax import lax
from jax.experimental import pallas as pl
from jax.experimental.pallas import tpu as pltpu
from jax.sharding import PartitionSpec as P

leak_slope = 0.2
bf16 = jnp.bfloat16
f32 = jnp.float32


def dot(a, b):
    return lax.dot_general(a, b, (((1,), (0,)), ((), ())), preferred_element_type=f32)


wide = 10240


def prep_kernel(first_ref, second_ref, out_ref):
    for block in range(64):
        sw, sd, ed, eh, ew, sh = [(block >> bit) & 1 for bit in (5, 4, 3, 2, 1, 0)]
        k = ((2 + sd - 2 * ed) * 4 + (2 + sh - 2 * eh)) * 4 + (2 + sw - 2 * ew)
        out_ref[:, block * 128:block * 128 + 128] = first_ref[:, k * 128:k * 128 + 128].astype(bf16)
    lane = lax.broadcasted_iota(jnp.int32, (16, 128), 1)
    for block in range(32):
        ed, eh, ew, sw, sd = (block >> 4) & 1, (block >> 3) & 1, (block >> 2) & 1, (block >> 1) & 1, block & 1
        parts = []
        for slot in range(2):
            sh = slot if sw == 0 else 1 - slot
            k = ((2 + sd - 2 * ed) * 4 + (2 + sh - 2 * eh)) * 4 + (2 + sw - 2 * ew)
            v = second_ref[:, (k // 2) * 128:(k // 2) * 128 + 128]
            parts.append(v if k % 2 == slot else pltpu.roll(v, 64, 1))
        v = jnp.where(lane < 64, parts[0], parts[1]).astype(bf16)
        row, col = (block // 16) * 16, 8192 + (block % 16) * 128
        out_ref[row:row + 16, col:col + 128] = v


def pack(gen_first, gen_second, interpret=False):
    vm = pl.BlockSpec(memory_space=pltpu.VMEM)
    return pl.pallas_call(
        prep_kernel,
        in_specs=[vm, vm],
        out_specs=vm,
        out_shape=jax.ShapeDtypeStruct((32, wide), bf16),
        interpret=interpret,
        name="pack",
    )(gen_first, gen_second)


def piece_copies(idx, pieces, w1, w2):
    first, second = [], []
    for n, src in enumerate(pieces):
        base = pl.multiple_of(idx[n] * 32, 32)
        first.append((src.at[:, pl.ds(0, 8192)], w1.at[pl.ds(base, 32), :]))
        base = pl.multiple_of(idx[n] * 16, 16)
        for part in range(2):
            second.append((src.at[pl.ds(16 * part, 16), pl.ds(8192, 2048)],
                           w2.at[pl.ds(base, 16), pl.ds(part * 2048, 2048)]))
    return first, second


def eval_kernel(idx, x_ref, crit_hbm, *refs):
    pieces, out_ref = refs[:8], refs[-18]
    (w1_ref, w2_ref, crit_ref, xa, hp, hs0, hs1, d0, d1, zb, cr, cb, tmp, pre, sem1, sem2, sem3) = refs[-17:]
    edge = [idx[8], idx[9]]
    row3 = lambda n, lanes: lax.broadcasted_iota(jnp.int32, (n, 16, lanes), 1)

    first, second = piece_copies(idx, pieces, w1_ref, w2_ref)
    first = [pltpu.make_async_copy(a, b, sem1.at[n]) for n, (a, b) in enumerate(first)]
    second_copies = [pltpu.make_async_copy(a, b, sem2.at[n]) for n, (a, b) in enumerate(second)]
    crit_copy = pltpu.make_async_copy(crit_hbm, crit_ref, sem3.at[0])
    for c in first + second_copies + [crit_copy]:
        c.start()

    zrow = jnp.zeros((16, 256), bf16)
    for v in range(4):
        for p in range(4):
            xa[v, p, 0] = zrow
            xa[v, p, 17] = zrow
    for p in range(4):
        x = x_ref[p].astype(f32)
        r = row3(16, 256)
        rolled = pltpu.roll(x, 1, 1)
        xa[0, p, 1:17] = rolled.astype(bf16)
        xa[1, p, 1:17] = jnp.where(r == 0, 0.0, x).astype(bf16)
        xa[2, p, 1:17] = jnp.where(r == 0, 0.0, rolled).astype(bf16)
        xa[3, p, 1:17] = x_ref[p]

    for c in first:
        c.wait()

    r = row3(51, 128)
    for sw in range(2):
        lhs = jnp.concatenate(
            [xa[sw * 2 + ew, ed:ed + 3, eh:eh + 17].reshape(816, 256)
             for ed in range(2) for eh in range(2) for ew in range(2)], axis=1)
        for sd in range(2):
            group = sw * 2 + sd
            rhs = []
            for ed in range(2):
                for eh in range(2):
                    for ew in range(2):
                        block = group * 8 + ed * 4 + eh * 2 + ew
                        rhs.append(w1_ref[:, block * 256:block * 256 + 256])
            res = jnp.maximum(dot(lhs, jnp.concatenate(rhs, axis=0)), 0.0)
            for sh in range(2):
                o = res[:, sh * 128:sh * 128 + 128].reshape(51, 16, 128)
                plain = o.astype(bf16)
                cleared = jnp.where(r == 0, 0.0, o).astype(bf16)
                if sw == 0:
                    places = ((hs0, 0, plain), (hs1, 0, cleared), (hp, 128, pltpu.roll(o, 15, 1).astype(bf16)))
                else:
                    places = ((hs0, 128, cleared), (hs1, 128, plain), (hp, 0, plain))
                for ref, lane, value in places:
                    for j in range(51):
                        ref[2 * (j // 17) + sd, 2 * (j % 17) + sh, :, lane:lane + 128] = value[j]
    for h in (hp, hs0, hs1):
        for p in range(6):
            h[p, 0] = zrow
            h[p, 33] = zrow

    @pl.when(edge[0] == 1)
    def _():
        for h in (hp, hs0, hs1):
            h[0] = jnp.zeros((34, 16, 256), bf16)

    @pl.when(edge[1] == 1)
    def _():
        for h in (hp, hs0, hs1):
            h[5] = jnp.zeros((34, 16, 256), bf16)

    for c in second_copies:
        c.wait()

    lane = lax.broadcasted_iota(jnp.int32, (16, 128), 1)
    top = lax.broadcasted_iota(jnp.int32, (16, 128), 0) == 0

    def products(jd, a):
        for s in range(2):
            h = hp if a == 1 else (hs0, hs1)[s]
            lhs = jnp.concatenate(
                [h[jd + ed, eh:eh + 33].reshape(528, 256) for ed in range(2) for eh in range(2)], axis=1)
            parts = []
            for e in range(4):
                for ew in range(2):
                    c = ((e * 2 + ew) * 2 + s) * 256
                    parts.append(w2_ref[:, c:c + 256])
            pre[a, s] = dot(lhs, jnp.concatenate(parts, axis=0))

    def images(jd, a):
        dst = d0 if a == 0 else d1
        for j in range(33):
            for sd in range(2):
                p = 2 * jd + sd
                u0 = jnp.tanh(pre[a, 0, j * 16:j * 16 + 16, sd * 128:sd * 128 + 128])
                u1 = jnp.tanh(pre[a, 1, j * 16:j * 16 + 16, sd * 128:sd * 128 + 128])
                if a == 0:
                    zb[p, j:j + 1, :] = u0[0:1, :]
                    u0 = jnp.where(top, 0.0, u0)
                dst[p, j, :, 0:128] = jnp.where(lane < 64, u0, u1).astype(bf16)
                dst[p, j, :, 128:256] = jnp.where(lane < 64, u1, u0).astype(bf16)

    def second_layer(jd, _):
        images(jnp.maximum(jd - 1, 0), 0)
        images(jnp.maximum(jd - 1, 0), 1)
        products(jd, 0)
        products(jd, 1)
        return 0

    lax.fori_loop(0, 5, second_layer, 0)
    images(4, 0)
    images(4, 1)
    z64 = jnp.zeros((1, 64), f32)
    for p in range(10):
        zb[p, 0:1, 0:64] = z64
        zb[p, 32:33, 64:128] = z64
    crit_copy.wait()
    for kd in range(4):
        for kh in range(4):
            g, sh = kh // 2, kh % 2
            for slot in range(2):
                kw = slot if sh == 0 else 1 - slot
                base = (kd * 4 + kh) * 256
                r0 = sh * 128 + slot * 64
                for half in range(2):
                    src = base + (half * 2 + kw) * 64
                    cr[kd * 2 + g, r0:r0 + 64, half * 128:half * 128 + 128] = crit_ref[src:src + 64, :]
            src = (kd * 4 + kh) * 256 + 128
            dst = (kd * 2 + g) * 128 + sh * 64
            cb[dst:dst + 64, :] = crit_ref[src:src + 64, :]
    z128 = jnp.zeros((16, 128), bf16)
    for d in (d0, d1):
        for p in range(10):
            d[p, 0, :, 0:128] = z128
            d[p, 32, :, 128:256] = z128

    @pl.when(edge[0] == 1)
    def _():
        for d in (d0, d1):
            d[0] = jnp.zeros((33, 16, 256), bf16)
        zb[0] = jnp.zeros((40, 128), f32)

    @pl.when(edge[1] == 1)
    def _():
        for d in (d0, d1):
            d[9] = jnp.zeros((33, 16, 256), bf16)
        zb[9] = jnp.zeros((40, 128), f32)

    def judge(y, _):
        def lhs(d):
            return jnp.concatenate(
                [d[2 * y + kd, g:g + 32].reshape(512, 256) for kd in range(4) for g in range(2)], axis=1)

        w = cr[...].reshape(2048, 256)
        acc0 = dot(lhs(d0), w)
        acc1 = dot(lhs(d1), w)
        bl = jnp.concatenate(
            [zb[2 * y + kd, g:g + 32, :].astype(bf16) for kd in range(4) for g in range(2)], axis=1)
        past = dot(bl, cb[...])
        even = acc0[:, 0:128] + acc1[:, 128:256]
        side = pltpu.roll(acc0[:, 128:256].reshape(32, 16, 128), 15, 1)
        side = jnp.where(row3(32, 128) == 15, past[:, None, :], side)
        odd = acc1[:, 0:128] + side.reshape(512, 128)
        tmp[pl.ds(0, 512, 2), :] = jnp.where(even > 0, even, leak_slope * even)
        tmp[pl.ds(1, 512, 2), :] = jnp.where(odd > 0, odd, leak_slope * odd)
        out_ref[0, y] = tmp[...].astype(bf16).reshape(32, 32, 128)
        return 0

    lax.fori_loop(0, 4, judge, 0)


def evaluate(idx, planes, crit, pieces, prev=None, interpret=False):
    vm = pl.BlockSpec(memory_space=pltpu.VMEM)
    hbm = pl.BlockSpec(memory_space=pl.ANY)
    which = 0 if prev is None else 1
    extra = [] if prev is None else [prev]
    return pl.pallas_call(
        eval_kernel,
        grid=(1,),
        in_specs=[pl.BlockSpec(memory_space=pltpu.SMEM), vm, hbm] + [hbm] * (8 + which),
        out_specs=pl.BlockSpec((1, 4, 32, 32, 128), lambda i: (which, 0, 0, 0, 0)),
        out_shape=jax.ShapeDtypeStruct((2, 4, 32, 32, 128), bf16),
        input_output_aliases={11: 0} if which else {},
        scratch_shapes=[
            pltpu.VMEM((256, 8192), bf16),
            pltpu.VMEM((128, 4096), bf16),
            pltpu.VMEM((4096, 128), bf16),
            pltpu.VMEM((4, 4, 18, 16, 256), bf16),
            pltpu.VMEM((6, 34, 16, 256), bf16),
            pltpu.VMEM((6, 34, 16, 256), bf16),
            pltpu.VMEM((6, 34, 16, 256), bf16),
            pltpu.VMEM((10, 33, 16, 256), bf16),
            pltpu.VMEM((10, 33, 16, 256), bf16),
            pltpu.VMEM((10, 40, 128), f32),
            pltpu.VMEM((8, 256, 256), bf16),
            pltpu.VMEM((1024, 128), bf16),
            pltpu.VMEM((1024, 128), f32),
            pltpu.VMEM((2, 2, 528, 256), f32),
            pltpu.SemaphoreType.DMA((8,)),
            pltpu.SemaphoreType.DMA((16,)),
            pltpu.SemaphoreType.DMA((1,)),
        ],
        compiler_params=pltpu.CompilerParams(vmem_limit_bytes=34 << 20),
        interpret=interpret,
        name="evaluate",
    )(idx, planes, crit, *pieces, *extra)


def shift(value, axis, step):
    count = lax.axis_size(axis)
    pairs = [(i, i + step) for i in range(count) if 0 <= i + step < count]
    return lax.ppermute(value, axis, pairs)


def exchange(offset, value):
    count = lax.axis_size("trainer")

    def branch(m):
        return lambda v: lax.ppermute(v, "trainer", [(i, i ^ m) for i in range(count)])

    return lax.switch(offset - 1, [branch(m) for m in range(1, count)], value)


def ring(value, step):
    return lax.ppermute(value, "depth", [(i, (i & 4) | ((i + step) & 3)) for i in range(8)])


def other(value):
    return lax.ppermute(value, "depth", [(i, i ^ 4) for i in range(8)])


def slant(value):
    return lax.ppermute(value, "depth", [(i, ((i & 4) ^ 4) | ((i - 1) & 3)) for i in range(8)])


def local(latent, gen_first, gen_second, critic, partner):
    offset = partner[0]
    depth = lax.axis_index("depth")
    last = lax.axis_size("depth") - 1
    row, at = depth & 4, depth & 3
    low_at, high_at, far_at = row | ((at + 3) & 3), row | ((at + 1) & 3), row | ((at + 2) & 3)
    idx = jnp.stack([depth, low_at, high_at, far_at, depth ^ 4, low_at ^ 4, high_at ^ 4, far_at ^ 4,
                     (depth == 0).astype(jnp.int32), (depth == last).astype(jnp.int32)])
    s0 = pack(gen_first[0], gen_second[0])
    a1, a3, b0 = ring(s0, 1), ring(s0, -1), other(s0)
    low = shift(latent[0, -1:], "depth", 1)
    high = shift(latent[0, :1], "depth", -1)
    mate_s0 = exchange(offset, s0)
    a1, a3, b0, low, high, mate_s0 = lax.optimization_barrier((a1, a3, b0, low, high, mate_s0))
    planes = jnp.concatenate([low, latent[0], high], axis=0)
    a2, b3, b1 = ring(a1, 1), ring(b0, -1), other(a1)
    mate_a1, mate_a3 = ring(mate_s0, 1), ring(mate_s0, -1)
    mate_b0 = exchange(offset, b0)
    a2, b3, b1, mate_b0, planes = lax.optimization_barrier((a2, b3, b1, mate_b0, planes))
    b2 = other(a2)
    mate_b1, mate_b3 = ring(mate_b0, 1), ring(mate_b0, -1)
    mate_a2, mate_b2 = ring(mate_a1, 1), slant(mate_a3)
    own = evaluate(idx, planes, critic[0], (s0, a1, a3, a2, b0, b1, b3, b2))
    mate_pieces = (mate_s0, mate_a1, mate_a3, mate_a2, mate_b0, mate_b1, mate_b3, mate_b2)
    return evaluate(idx, planes, critic[0], mate_pieces, own)[None]


def solution(mesh):
    in_specs = (
        P("trainer", "depth", None, None, None),
        P("trainer", "depth", None),
        P("trainer", "depth", None),
        P("trainer", None, None),
        P(),
    )
    out_specs = P("trainer", None, "depth", None, None, None)
    return jax.shard_map(local, mesh=mesh, in_specs=in_specs, out_specs=out_specs, check_vma=False)
```

```python
import functools

import jax
import jax.numpy as jnp
from jax import lax
from jax.experimental import pallas as pl
from jax.experimental.pallas import tpu as pltpu
from jax.sharding import PartitionSpec as P


leak_slope = 0.2
bf16 = jnp.bfloat16
f32 = jnp.float32


def dot(a, b):
    return lax.dot_general(a, b, (((1,), (0,)), ((), ())), preferred_element_type=f32)


wide = 10240


def prep_kernel(first_ref, second_ref, out_ref):
    for block in range(64):
        sw, sd, ed, eh, ew, sh = [(block >> bit) & 1 for bit in (5, 4, 3, 2, 1, 0)]
        k = ((2 + sd - 2 * ed) * 4 + (2 + sh - 2 * eh)) * 4 + (2 + sw - 2 * ew)
        out_ref[:, block * 128:block * 128 + 128] = first_ref[:, k * 128:k * 128 + 128].astype(bf16)
    lane = lax.broadcasted_iota(jnp.int32, (16, 128), 1)
    for block in range(32):
        ed, eh, ew, sw, sd = (block >> 4) & 1, (block >> 3) & 1, (block >> 2) & 1, (block >> 1) & 1, block & 1
        parts = []
        for slot in range(2):
            sh = slot if sw == 0 else 1 - slot
            k = ((2 + sd - 2 * ed) * 4 + (2 + sh - 2 * eh)) * 4 + (2 + sw - 2 * ew)
            v = second_ref[:, (k // 2) * 128:(k // 2) * 128 + 128]
            parts.append(v if k % 2 == slot else pltpu.roll(v, 64, 1))
        v = jnp.where(lane < 64, parts[0], parts[1]).astype(bf16)
        row, col = (block // 16) * 16, 8192 + (block % 16) * 128
        out_ref[row:row + 16, col:col + 128] = v


def pack(gen_first, gen_second, interpret=False):
    vm = pl.BlockSpec(memory_space=pltpu.VMEM)
    return pl.pallas_call(
        prep_kernel,
        in_specs=[vm, vm],
        out_specs=vm,
        out_shape=jax.ShapeDtypeStruct((32, wide), bf16),
        interpret=interpret,
        name="pack",
    )(gen_first, gen_second)


def piece_copies(idx, pieces, w1, w2):
    first, second = [], []
    for half in range(2):
        cols = pl.ds(half * 4096, 4096)
        for n, src in enumerate(pieces):
            base = pl.multiple_of(idx[n] * 32, 32)
            first.append((src.at[:, cols], w1.at[pl.ds(base, 32), cols]))
    for n, src in enumerate(pieces):
        base = pl.multiple_of(idx[n] * 16, 16)
        for part in range(2):
            second.append((src.at[pl.ds(16 * part, 16), pl.ds(8192, 2048)],
                           w2.at[pl.ds(base, 16), pl.ds(part * 2048, 2048)]))
    return first, second


def eval_kernel(which, idx, low_ref, mid_ref, high_ref, crit_hbm, *refs):
    pieces, out_ref = refs[:8], refs[-20]
    (w1_ref, w2_ref, crit_ref, xa, hp, hs0, hs1, d0, d1, zb, cr, cb, tmp, pre, ready, sem1, sem2, sem3, sem4) = refs[-19:]
    edge = [idx[8], idx[9]]
    row3 = lambda n, lanes: lax.broadcasted_iota(jnp.int32, (n, 16, lanes), 1)

    first, second = piece_copies(idx, pieces, w1_ref, w2_ref)
    first = [pltpu.make_async_copy(a, b, sem1.at[n]) for n, (a, b) in enumerate(first)]
    second_copies = [pltpu.make_async_copy(a, b, sem2.at[n]) for n, (a, b) in enumerate(second)]
    crit_copy = pltpu.make_async_copy(crit_hbm, crit_ref, sem3.at[0])
    for c in first[:8]:
        c.start()

    zrow = jnp.zeros((16, 256), bf16)
    for v in range(4):
        for p in range(4):
            xa[v, p, 0] = zrow
            xa[v, p, 17] = zrow
    for p, plane in enumerate((low_ref[0], mid_ref[0], mid_ref[1], high_ref[0])):
        x = plane.astype(f32)
        r = row3(16, 256)
        rolled = pltpu.roll(x, 1, 1)
        xa[0, p, 1:17] = rolled.astype(bf16)
        xa[1, p, 1:17] = jnp.where(r == 0, 0.0, x).astype(bf16)
        xa[2, p, 1:17] = jnp.where(r == 0, 0.0, rolled).astype(bf16)
        xa[3, p, 1:17] = plane

    r = row3(51, 128)
    for sw in range(2):
        for c in first[sw * 8:sw * 8 + 8]:
            c.wait()
        for c in (first[8:], second_copies + [crit_copy])[sw]:
            c.start()
        lhs = jnp.concatenate(
            [xa[sw * 2 + ew, ed:ed + 3, eh:eh + 17].reshape(816, 256)
             for ed in range(2) for eh in range(2) for ew in range(2)], axis=1)
        for sd in range(2):
            group = sw * 2 + sd
            rhs = []
            for ed in range(2):
                for eh in range(2):
                    for ew in range(2):
                        block = group * 8 + ed * 4 + eh * 2 + ew
                        rhs.append(w1_ref[:, block * 256:block * 256 + 256])
            res = jnp.maximum(dot(lhs, jnp.concatenate(rhs, axis=0)), 0.0)
            for sh in range(2):
                o = res[:, sh * 128:sh * 128 + 128].reshape(51, 16, 128)
                plain = o.astype(bf16)
                cleared = jnp.where(r == 0, 0.0, o).astype(bf16)
                if sw == 0:
                    places = ((hs0, 0, plain), (hs1, 0, cleared), (hp, 128, pltpu.roll(o, 15, 1).astype(bf16)))
                else:
                    places = ((hs0, 128, cleared), (hs1, 128, plain), (hp, 0, plain))
                for ref, lane, value in places:
                    for j in range(51):
                        ref[2 * (j // 17) + sd, 2 * (j % 17) + sh, :, lane:lane + 128] = value[j]
    for h in (hp, hs0, hs1):
        for p in range(6):
            h[p, 0] = zrow
            h[p, 33] = zrow

    @pl.when(edge[0] == 1)
    def _():
        for h in (hp, hs0, hs1):
            h[0] = jnp.zeros((34, 16, 256), bf16)

    @pl.when(edge[1] == 1)
    def _():
        for h in (hp, hs0, hs1):
            h[5] = jnp.zeros((34, 16, 256), bf16)

    for c in second_copies:
        c.wait()

    lane = lax.broadcasted_iota(jnp.int32, (16, 128), 1)
    top = lax.broadcasted_iota(jnp.int32, (16, 128), 0) == 0

    def products(jd, a):
        for s in range(2):
            h = hp if a == 1 else (hs0, hs1)[s]
            lhs = jnp.concatenate(
                [h[jd + ed, eh:eh + 33].reshape(528, 256) for ed in range(2) for eh in range(2)], axis=1)
            parts = []
            for e in range(4):
                for ew in range(2):
                    c = ((e * 2 + ew) * 2 + s) * 256
                    parts.append(w2_ref[:, c:c + 256])
            pre[a, s] = dot(lhs, jnp.concatenate(parts, axis=0))

    def images(jd, a):
        dst = d0 if a == 0 else d1
        for j in range(33):
            for sd in range(2):
                p = 2 * jd + sd
                u0 = jnp.tanh(pre[a, 0, j * 16:j * 16 + 16, sd * 128:sd * 128 + 128])
                u1 = jnp.tanh(pre[a, 1, j * 16:j * 16 + 16, sd * 128:sd * 128 + 128])
                if a == 0:
                    zb[p, j:j + 1, :] = u0[0:1, :]
                    u0 = jnp.where(top, 0.0, u0)
                dst[p, j, :, 0:128] = jnp.where(lane < 64, u0, u1).astype(bf16)
                dst[p, j, :, 128:256] = jnp.where(lane < 64, u1, u0).astype(bf16)

    for jd in range(6):
        for a in range(2):
            if jd > 0:
                images(jd - 1, a)
            if jd < 5:
                products(jd, a)
    z64 = jnp.zeros((1, 64), f32)
    for p in range(10):
        zb[p, 0:1, 0:64] = z64
        zb[p, 32:33, 64:128] = z64
    crit_copy.wait()
    for kd in range(4):
        for kh in range(4):
            g, sh = kh // 2, kh % 2
            for slot in range(2):
                kw = slot if sh == 0 else 1 - slot
                base = (kd * 4 + kh) * 256
                r0 = sh * 128 + slot * 64
                for half in range(2):
                    src = base + (half * 2 + kw) * 64
                    cr[kd * 2 + g, r0:r0 + 64, half * 128:half * 128 + 128] = crit_ref[src:src + 64, :]
            src = (kd * 4 + kh) * 256 + 128
            dst = (kd * 2 + g) * 128 + sh * 64
            cb[dst:dst + 64, :] = crit_ref[src:src + 64, :]
    z128 = jnp.zeros((16, 128), bf16)
    for d in (d0, d1):
        for p in range(10):
            d[p, 0, :, 0:128] = z128
            d[p, 32, :, 128:256] = z128

    @pl.when(edge[0] == 1)
    def _():
        for d in (d0, d1):
            d[0] = jnp.zeros((33, 16, 256), bf16)
        zb[0] = jnp.zeros((40, 128), f32)

    @pl.when(edge[1] == 1)
    def _():
        for d in (d0, d1):
            d[9] = jnp.zeros((33, 16, 256), bf16)
        zb[9] = jnp.zeros((40, 128), f32)

    def judge(y, _):
        def lhs(d):
            return jnp.concatenate(
                [jnp.concatenate([d[4 * y + 2 * v + kd, g:g + 32].reshape(512, 256) for v in range(2)], axis=0)
                 for kd in range(4) for g in range(2)], axis=1)

        w = cr[...].reshape(2048, 256)
        acc0 = dot(lhs(d0), w)
        acc1 = dot(lhs(d1), w)
        bl = jnp.concatenate(
            [jnp.concatenate([zb[4 * y + 2 * v + kd, g:g + 32, :].astype(bf16) for v in range(2)], axis=0)
             for kd in range(4) for g in range(2)], axis=1)
        past = dot(bl, cb[...])
        even = acc0[:, 0:128] + acc1[:, 128:256]
        side = pltpu.roll(acc0[:, 128:256].reshape(64, 16, 128), 15, 1)
        side = jnp.where(row3(64, 128) == 15, past[:, None, :], side)
        odd = acc1[:, 0:128] + side.reshape(1024, 128)
        tmp[pl.ds(0, 1024, 2), :] = jnp.where(even > 0, even, leak_slope * even)
        tmp[pl.ds(1, 1024, 2), :] = jnp.where(odd > 0, odd, leak_slope * odd)
        ready[y] = tmp[...].astype(bf16).reshape(2, 32, 32, 128)
        pltpu.make_async_copy(ready.at[y], out_ref.at[which, pl.ds(2 * y, 2)], sem4.at[y]).start()
        return 0

    lax.fori_loop(0, 2, judge, 0)
    for y in range(2):
        pltpu.make_async_copy(ready.at[y], out_ref.at[which, pl.ds(2 * y, 2)], sem4.at[y]).wait()


def evaluate(idx, low, mid, high, crit, pieces, prev=None, interpret=False):
    vm = pl.BlockSpec(memory_space=pltpu.VMEM)
    hbm = pl.BlockSpec(memory_space=pl.ANY)
    which = 0 if prev is None else 1
    extra = [] if prev is None else [prev]
    return pl.pallas_call(
        functools.partial(eval_kernel, which),
        in_specs=[pl.BlockSpec(memory_space=pltpu.SMEM), vm, vm, vm, hbm] + [hbm] * (8 + which),
        out_specs=hbm,
        out_shape=jax.ShapeDtypeStruct((2, 4, 32, 32, 128), bf16),
        input_output_aliases={13: 0} if which else {},
        scratch_shapes=[
            pltpu.VMEM((256, 8192), bf16),
            pltpu.VMEM((128, 4096), bf16),
            pltpu.VMEM((4096, 128), bf16),
            pltpu.VMEM((4, 4, 18, 16, 256), bf16),
            pltpu.VMEM((6, 34, 16, 256), bf16),
            pltpu.VMEM((6, 34, 16, 256), bf16),
            pltpu.VMEM((6, 34, 16, 256), bf16),
            pltpu.VMEM((10, 33, 16, 256), bf16),
            pltpu.VMEM((10, 33, 16, 256), bf16),
            pltpu.VMEM((10, 40, 128), f32),
            pltpu.VMEM((8, 256, 256), bf16),
            pltpu.VMEM((1024, 128), bf16),
            pltpu.VMEM((2048, 128), f32),
            pltpu.VMEM((2, 2, 528, 256), f32),
            pltpu.VMEM((2, 2, 32, 32, 128), bf16),
            pltpu.SemaphoreType.DMA((16,)),
            pltpu.SemaphoreType.DMA((16,)),
            pltpu.SemaphoreType.DMA((1,)),
            pltpu.SemaphoreType.DMA((2,)),
        ],
        compiler_params=pltpu.CompilerParams(vmem_limit_bytes=34 << 20),
        interpret=interpret,
        name="evaluate",
    )(idx, low, mid, high, crit, *pieces, *extra)


def shift(value, axis, step):
    count = lax.axis_size(axis)
    pairs = [(i, i + step) for i in range(count) if 0 <= i + step < count]
    return lax.ppermute(value, axis, pairs)


def exchange(offset, value):
    count = lax.axis_size("trainer")

    def branch(m):
        return lambda v: lax.ppermute(v, "trainer", [(i, i ^ m) for i in range(count)])

    return lax.switch(offset - 1, [branch(m) for m in range(1, count)], value)


def ring(value, step):
    return lax.ppermute(value, "depth", [(i, (i & 4) | ((i + step) & 3)) for i in range(8)])


def other(value):
    return lax.ppermute(value, "depth", [(i, i ^ 4) for i in range(8)])


def slant(value):
    return lax.ppermute(value, "depth", [(i, ((i & 4) ^ 4) | ((i - 1) & 3)) for i in range(8)])


def local(latent, gen_first, gen_second, critic, partner):
    offset = partner[0]
    depth = lax.axis_index("depth")
    last = lax.axis_size("depth") - 1
    row, at = depth & 4, depth & 3
    low_at, high_at, far_at = row | ((at + 3) & 3), row | ((at + 1) & 3), row | ((at + 2) & 3)
    idx = jnp.stack([depth, low_at, high_at, far_at, depth ^ 4, low_at ^ 4, high_at ^ 4, far_at ^ 4,
                     (depth == 0).astype(jnp.int32), (depth == last).astype(jnp.int32)])
    s0 = pack(gen_first[0], gen_second[0])
    a1, a3, b0 = ring(s0, 1), ring(s0, -1), other(s0)
    mate_s0 = exchange(offset, s0)
    a1, a3, b0, mate_s0 = lax.optimization_barrier((a1, a3, b0, mate_s0))
    a2, b3, b1 = ring(a1, 1), ring(b0, -1), other(a1)
    mate_a1, mate_a3 = ring(mate_s0, 1), ring(mate_s0, -1)
    mate_b0 = exchange(offset, b0)
    a2, b3, b1, mate_b0, mid = lax.optimization_barrier((a2, b3, b1, mate_b0, latent[0]))
    b2 = other(a2)
    low = shift(mid[-1:], "depth", 1)
    high = shift(mid[:1], "depth", -1)
    mate_a2 = ring(mate_a1, 1)
    mate_b2 = slant(mate_a3)
    mate_b1 = ring(mate_b0, 1)
    mate_b3 = ring(mate_b0, -1)
    own = evaluate(idx, low, mid, high, critic[0], (s0, a1, a3, a2, b0, b1, b3, b2))
    mate_pieces = (mate_s0, mate_a1, mate_a3, mate_a2, mate_b0, mate_b1, mate_b3, mate_b2)
    return evaluate(idx, low, mid, high, critic[0], mate_pieces, own)[None]


def solution(mesh):
    in_specs = (
        P("trainer", "depth", None, None, None),
        P("trainer", "depth", None),
        P("trainer", "depth", None),
        P("trainer", None, None),
        P(),
    )
    out_specs = P("trainer", None, "depth", None, None, None)
    return jax.shard_map(local, mesh=mesh, in_specs=in_specs, out_specs=out_specs, check_vma=False)
```

```python
import functools

import jax
import jax.numpy as jnp
from jax import lax
from jax.experimental import pallas as pl
from jax.experimental.pallas import tpu as pltpu
from jax.sharding import PartitionSpec as P


leak_slope = 0.2
bf16 = jnp.bfloat16
f32 = jnp.float32


def dot(a, b):
    return lax.dot_general(a, b, (((1,), (0,)), ((), ())), preferred_element_type=f32)


wide = 10240


def prep_kernel(first_ref, second_ref, out_ref):
    for block in range(64):
        sw, sd, ed, eh, ew, sh = [(block >> bit) & 1 for bit in (5, 4, 3, 2, 1, 0)]
        k = ((2 + sd - 2 * ed) * 4 + (2 + sh - 2 * eh)) * 4 + (2 + sw - 2 * ew)
        out_ref[:, block * 128:block * 128 + 128] = first_ref[:, k * 128:k * 128 + 128].astype(bf16)
    lane = lax.broadcasted_iota(jnp.int32, (16, 128), 1)
    for block in range(32):
        ed, eh, ew, sw, sd = (block >> 4) & 1, (block >> 3) & 1, (block >> 2) & 1, (block >> 1) & 1, block & 1
        parts = []
        for slot in range(2):
            sh = slot if sw == 0 else 1 - slot
            k = ((2 + sd - 2 * ed) * 4 + (2 + sh - 2 * eh)) * 4 + (2 + sw - 2 * ew)
            v = second_ref[:, (k // 2) * 128:(k // 2) * 128 + 128]
            parts.append(v if k % 2 == slot else pltpu.roll(v, 64, 1))
        v = jnp.where(lane < 64, parts[0], parts[1]).astype(bf16)
        row, col = (block // 16) * 16, 8192 + (block % 16) * 128
        out_ref[row:row + 16, col:col + 128] = v


def pack(gen_first, gen_second, interpret=False):
    vm = pl.BlockSpec(memory_space=pltpu.VMEM)
    return pl.pallas_call(
        prep_kernel,
        in_specs=[vm, vm],
        out_specs=vm,
        out_shape=jax.ShapeDtypeStruct((32, wide), bf16),
        interpret=interpret,
        name="pack",
    )(gen_first, gen_second)


def piece_copies(idx, pieces, w1, w2):
    first, second = [], []
    for half in range(2):
        cols = pl.ds(half * 4096, 4096)
        for n, src in enumerate(pieces):
            base = pl.multiple_of(idx[n] * 32, 32)
            first.append((src.at[:, cols], w1.at[pl.ds(base, 32), cols]))
    for n, src in enumerate(pieces):
        base = pl.multiple_of(idx[n] * 16, 16)
        for part in range(2):
            second.append((src.at[pl.ds(16 * part, 16), pl.ds(8192, 2048)],
                           w2.at[pl.ds(base, 16), pl.ds(part * 2048, 2048)]))
    return first, second


def eval_kernel(which, idx, low_ref, mid_ref, high_ref, crit_hbm, *refs):
    pieces, out_ref = refs[:8], refs[-20]
    (w1_ref, w2_ref, crit_ref, xa, hp, hs0, hs1, d0, d1, zb, cr, cb, tmp, pre, ready, sem1, sem2, sem3, sem4) = refs[-19:]
    edge = [idx[8], idx[9]]
    row3 = lambda n, lanes: lax.broadcasted_iota(jnp.int32, (n, 16, lanes), 1)

    first, second = piece_copies(idx, pieces, w1_ref, w2_ref)
    first = [pltpu.make_async_copy(a, b, sem1.at[n]) for n, (a, b) in enumerate(first)]
    second_copies = [pltpu.make_async_copy(a, b, sem2.at[n]) for n, (a, b) in enumerate(second)]
    crit_copy = pltpu.make_async_copy(crit_hbm, crit_ref, sem3.at[0])
    for c in first[:8]:
        c.start()

    zrow = jnp.zeros((16, 256), bf16)
    for v in range(4):
        for p in range(4):
            xa[v, p, 0] = zrow
            xa[v, p, 17] = zrow
    for p, plane in enumerate((low_ref[0], mid_ref[0], mid_ref[1], high_ref[0])):
        x = plane.astype(f32)
        r = row3(16, 256)
        rolled = pltpu.roll(x, 1, 1)
        xa[0, p, 1:17] = rolled.astype(bf16)
        xa[1, p, 1:17] = jnp.where(r == 0, 0.0, x).astype(bf16)
        xa[2, p, 1:17] = jnp.where(r == 0, 0.0, rolled).astype(bf16)
        xa[3, p, 1:17] = plane

    r = row3(51, 128)
    for sw in range(2):
        for c in first[sw * 8:sw * 8 + 8]:
            c.wait()
        for c in (first[8:], second_copies + [crit_copy])[sw]:
            c.start()
        lhs = jnp.concatenate(
            [xa[sw * 2 + ew, ed:ed + 3, eh:eh + 17].reshape(816, 256)
             for ed in range(2) for eh in range(2) for ew in range(2)], axis=1)
        for sd in range(2):
            group = sw * 2 + sd
            rhs = []
            for ed in range(2):
                for eh in range(2):
                    for ew in range(2):
                        block = group * 8 + ed * 4 + eh * 2 + ew
                        rhs.append(w1_ref[:, block * 256:block * 256 + 256])
            res = jnp.maximum(dot(lhs, jnp.concatenate(rhs, axis=0)), 0.0)
            for sh in range(2):
                o = res[:, sh * 128:sh * 128 + 128].reshape(51, 16, 128)
                plain = o.astype(bf16)
                cleared = jnp.where(r == 0, 0.0, o).astype(bf16)
                if sw == 0:
                    places = ((hs0, 0, plain), (hs1, 0, cleared), (hp, 128, pltpu.roll(o, 15, 1).astype(bf16)))
                else:
                    places = ((hs0, 128, cleared), (hs1, 128, plain), (hp, 0, plain))
                for ref, lane, value in places:
                    for j in range(51):
                        ref[2 * (j // 17) + sd, 2 * (j % 17) + sh, :, lane:lane + 128] = value[j]
    for h in (hp, hs0, hs1):
        for p in range(6):
            h[p, 0] = zrow
            h[p, 33] = zrow

    @pl.when(edge[0] == 1)
    def _():
        for h in (hp, hs0, hs1):
            h[0] = jnp.zeros((34, 16, 256), bf16)

    @pl.when(edge[1] == 1)
    def _():
        for h in (hp, hs0, hs1):
            h[5] = jnp.zeros((34, 16, 256), bf16)

    for c in second_copies:
        c.wait()

    crit_copy.wait()
    for kd in range(4):
        for kh in range(4):
            g, sh = kh // 2, kh % 2
            for slot in range(2):
                kw = slot if sh == 0 else 1 - slot
                base = (kd * 4 + kh) * 256
                r0 = sh * 128 + slot * 64
                for half in range(2):
                    src = base + (half * 2 + kw) * 64
                    cr[kd * 2 + g, r0:r0 + 64, half * 128:half * 128 + 128] = crit_ref[src:src + 64, :]
            src = (kd * 4 + kh) * 256 + 128
            dst = (kd * 2 + g) * 128 + sh * 64
            cb[dst:dst + 64, :] = crit_ref[src:src + 64, :]

    lane = lax.broadcasted_iota(jnp.int32, (16, 128), 1)
    top = lax.broadcasted_iota(jnp.int32, (16, 128), 0) == 0

    def products(jd, a):
        for s in range(2):
            h = hp if a == 1 else (hs0, hs1)[s]
            lhs = jnp.concatenate(
                [h[jd + ed, eh:eh + 33].reshape(528, 256) for ed in range(2) for eh in range(2)], axis=1)
            parts = []
            for e in range(4):
                for ew in range(2):
                    c = ((e * 2 + ew) * 2 + s) * 256
                    parts.append(w2_ref[:, c:c + 256])
            pre[a, s] = dot(lhs, jnp.concatenate(parts, axis=0))

    def images(jd, a):
        dst = d0 if a == 0 else d1
        for j in range(33):
            for sd in range(2):
                p = 2 * jd + sd
                u0 = jnp.tanh(pre[a, 0, j * 16:j * 16 + 16, sd * 128:sd * 128 + 128])
                u1 = jnp.tanh(pre[a, 1, j * 16:j * 16 + 16, sd * 128:sd * 128 + 128])
                if a == 0:
                    zb[p, j:j + 1, :] = u0[0:1, :]
                    u0 = jnp.where(top, 0.0, u0)
                dst[p, j, :, 0:128] = jnp.where(lane < 64, u0, u1).astype(bf16)
                dst[p, j, :, 128:256] = jnp.where(lane < 64, u1, u0).astype(bf16)

    for jd in range(6):
        for a in range(2):
            if jd > 0:
                images(jd - 1, a)
            if jd < 5:
                products(jd, a)
    z64 = jnp.zeros((1, 64), f32)
    for p in range(10):
        zb[p, 0:1, 0:64] = z64
        zb[p, 32:33, 64:128] = z64
    z128 = jnp.zeros((16, 128), bf16)
    for d in (d0, d1):
        for p in range(10):
            d[p, 0, :, 0:128] = z128
            d[p, 32, :, 128:256] = z128

    @pl.when(edge[0] == 1)
    def _():
        for d in (d0, d1):
            d[0] = jnp.zeros((33, 16, 256), bf16)
        zb[0] = jnp.zeros((40, 128), f32)

    @pl.when(edge[1] == 1)
    def _():
        for d in (d0, d1):
            d[9] = jnp.zeros((33, 16, 256), bf16)
        zb[9] = jnp.zeros((40, 128), f32)

    def judge(y, _):
        def lhs(d):
            return jnp.concatenate(
                [jnp.concatenate([d[4 * y + 2 * v + kd, g:g + 32].reshape(512, 256) for v in range(2)], axis=0)
                 for kd in range(4) for g in range(2)], axis=1)

        w = cr[...].reshape(2048, 256)
        acc0 = dot(lhs(d0), w)
        acc1 = dot(lhs(d1), w)
        bl = jnp.concatenate(
            [jnp.concatenate([zb[4 * y + 2 * v + kd, g:g + 32, :].astype(bf16) for v in range(2)], axis=0)
             for kd in range(4) for g in range(2)], axis=1)
        past = dot(bl, cb[...])
        even = acc0[:, 0:128] + acc1[:, 128:256]
        side = pltpu.roll(acc0[:, 128:256].reshape(64, 16, 128), 15, 1)
        side = jnp.where(row3(64, 128) == 15, past[:, None, :], side)
        odd = acc1[:, 0:128] + side.reshape(1024, 128)
        tmp[pl.ds(0, 1024, 2), :] = jnp.where(even > 0, even, leak_slope * even)
        tmp[pl.ds(1, 1024, 2), :] = jnp.where(odd > 0, odd, leak_slope * odd)
        ready[y] = tmp[...].astype(bf16).reshape(2, 32, 32, 128)
        pltpu.make_async_copy(ready.at[y], out_ref.at[which, pl.ds(2 * y, 2)], sem4.at[y]).start()
        return 0

    lax.fori_loop(0, 2, judge, 0)
    for y in range(2):
        pltpu.make_async_copy(ready.at[y], out_ref.at[which, pl.ds(2 * y, 2)], sem4.at[y]).wait()


def evaluate(idx, low, mid, high, crit, pieces, prev=None, interpret=False):
    vm = pl.BlockSpec(memory_space=pltpu.VMEM)
    hbm = pl.BlockSpec(memory_space=pl.ANY)
    which = 0 if prev is None else 1
    extra = [] if prev is None else [prev]
    return pl.pallas_call(
        functools.partial(eval_kernel, which),
        in_specs=[pl.BlockSpec(memory_space=pltpu.SMEM), vm, vm, vm, hbm] + [hbm] * (8 + which),
        out_specs=hbm,
        out_shape=jax.ShapeDtypeStruct((2, 4, 32, 32, 128), bf16),
        input_output_aliases={13: 0} if which else {},
        scratch_shapes=[
            pltpu.VMEM((256, 8192), bf16),
            pltpu.VMEM((128, 4096), bf16),
            pltpu.VMEM((4096, 128), bf16),
            pltpu.VMEM((4, 4, 18, 16, 256), bf16),
            pltpu.VMEM((6, 34, 16, 256), bf16),
            pltpu.VMEM((6, 34, 16, 256), bf16),
            pltpu.VMEM((6, 34, 16, 256), bf16),
            pltpu.VMEM((10, 33, 16, 256), bf16),
            pltpu.VMEM((10, 33, 16, 256), bf16),
            pltpu.VMEM((10, 40, 128), f32),
            pltpu.VMEM((8, 256, 256), bf16),
            pltpu.VMEM((1024, 128), bf16),
            pltpu.VMEM((2048, 128), f32),
            pltpu.VMEM((2, 2, 528, 256), f32),
            pltpu.VMEM((2, 2, 32, 32, 128), bf16),
            pltpu.SemaphoreType.DMA((16,)),
            pltpu.SemaphoreType.DMA((16,)),
            pltpu.SemaphoreType.DMA((1,)),
            pltpu.SemaphoreType.DMA((2,)),
        ],
        compiler_params=pltpu.CompilerParams(vmem_limit_bytes=60 << 20),
        interpret=interpret,
        name="evaluate",
    )(idx, low, mid, high, crit, *pieces, *extra)


def shift(value, axis, step):
    count = lax.axis_size(axis)
    pairs = [(i, i + step) for i in range(count) if 0 <= i + step < count]
    return lax.ppermute(value, axis, pairs)


def exchange(offset, value):
    count = lax.axis_size("trainer")

    def branch(m):
        return lambda v: lax.ppermute(v, "trainer", [(i, i ^ m) for i in range(count)])

    return lax.switch(offset - 1, [branch(m) for m in range(1, count)], value)


def ring(value, step):
    return lax.ppermute(value, "depth", [(i, (i & 4) | ((i + step) & 3)) for i in range(8)])


def other(value):
    return lax.ppermute(value, "depth", [(i, i ^ 4) for i in range(8)])


def slant(value):
    return lax.ppermute(value, "depth", [(i, ((i & 4) ^ 4) | ((i - 1) & 3)) for i in range(8)])


def local(latent, gen_first, gen_second, critic, partner):
    offset = partner[0]
    depth = lax.axis_index("depth")
    last = lax.axis_size("depth") - 1
    row, at = depth & 4, depth & 3
    low_at, high_at, far_at = row | ((at + 3) & 3), row | ((at + 1) & 3), row | ((at + 2) & 3)
    idx = jnp.stack([depth, low_at, high_at, far_at, depth ^ 4, low_at ^ 4, high_at ^ 4, far_at ^ 4,
                     (depth == 0).astype(jnp.int32), (depth == last).astype(jnp.int32)])
    s0 = pack(gen_first[0], gen_second[0])
    a1, a3, b0 = ring(s0, 1), ring(s0, -1), other(s0)
    mate_s0 = exchange(offset, s0)
    a1, a3, b0, mate_s0 = lax.optimization_barrier((a1, a3, b0, mate_s0))
    a2, b3, b1 = ring(a1, 1), ring(b0, -1), other(a1)
    mate_a1, mate_a3 = ring(mate_s0, 1), ring(mate_s0, -1)
    mate_b0 = other(mate_s0)
    a2, b3, b1, mid = lax.optimization_barrier((a2, b3, b1, latent[0]))
    b2 = ring(b1, 1)
    low = shift(mid[-1:], "depth", 1)
    high = shift(mid[:1], "depth", -1)
    mate_a2 = ring(mate_a1, 1)
    mate_b2 = slant(mate_a3)
    mate_b1 = other(mate_a1)
    mate_b3 = ring(mate_b0, -1)
    own = evaluate(idx, low, mid, high, critic[0], (s0, a1, a3, a2, b0, b1, b3, b2))
    mate_pieces = (mate_s0, mate_a1, mate_a3, mate_a2, mate_b0, mate_b1, mate_b3, mate_b2)
    return evaluate(idx, low, mid, high, critic[0], mate_pieces, own)[None]


def solution(mesh):
    in_specs = (
        P("trainer", "depth", None, None, None),
        P("trainer", "depth", None),
        P("trainer", "depth", None),
        P("trainer", None, None),
        P(),
    )
    out_specs = P("trainer", None, "depth", None, None, None)
    return jax.shard_map(local, mesh=mesh, in_specs=in_specs, out_specs=out_specs, check_vma=False)
```
